32 devices in a mesh: segment: 4 (over y, core), chan: 4 (over z), tm: 2 (over x).
Axes of the slice: x: 2, y: 2, z: 4, core: 2. Of those that a mesh axis runs over, the one named last changes fastest.
Arguments:
- voltages: bfloat16 [3, 512, 2048, 128], P(None, 'chan', ('segment', 'tm')), may hold values from -6 to 6
- flags: int32 [512], P('chan'), may hold values 0 or 1
- delays: int32 [512, 512], replicated, may hold values from 0 to 127
- analysis_taps: float32 [4, 64], replicated, may hold values from -3 to 3
- synthesis_taps: float32 [4, 64], replicated, may hold values from -3 to 3
Outputs:
- vis: float32 [64, 8, 2, 512, 512], P('chan', ('segment', 'tm'))
- beams: bfloat16 [3, 512, 2048, 128], P(None, 'chan', ('segment', 'tm'))
The draws below stay inside these ranges and needn't reach their ends.
All inputs are finite; a program needn't handle non-finite values. No bound on the sum of `flags` on one device may be relied on, other than what follows from the above.
Results may differ from the reference program's by a relative error of at most 0.008.
Values may be sent and summed in bfloat16 or wider, within the bound.
A program may use at most 256 MiB of HBM per device.

```python
import math
import jax
import jax.numpy as jnp
from jax import lax

A = 512
C = 64
B = 512
TAPS = 4
FB = 256
MB = 3
NBLK = 8
NT = 2048


def set_ends(result, stream_key, least, high):
    shape = result.shape
    spot = [jax.random.randint(jax.random.fold_in(stream_key, axis), (), 0, shape[axis]) for axis in range(len(shape))]
    result = result.at[tuple(spot)].set(least)
    longest = shape.index(max(shape))
    spot[longest] = (spot[longest] + 1) % shape[longest]
    return result.at[tuple(spot)].set(high)


def levels(own_key, dims, split, least, largest):
    def one(position, parts):
        draws = jax.random.uniform(jax.random.fold_in(jax.random.fold_in(own_key, 6), position), (parts,), jnp.float32, least / len(split), largest / len(split))
        return jnp.repeat(jnp.exp(draws), dims[position] // parts).reshape((-1,) + (1,) * (len(dims) - position - 1))

    level = one(*split[0])
    for cut in split[1:]:
        level = level * one(*cut)
    return level


def scatter_about(stream_key, shape, spread, most, split=(), kind=jnp.bfloat16):
    drawn = spread * jax.random.normal(stream_key, shape, jnp.float32)
    if split:
        drawn = drawn * levels(stream_key, shape, split, -0.22, 0.18)
    return jnp.clip(drawn, -most, most).astype(kind)


def setup_inputs(seed: int = 0) -> dict:
    seeds = jax.random.split(jax.random.key(seed), 6)
    return {
        "voltages": scatter_about(seeds[0], (MB, A, NT, 2 * C), 1.0, 6.0, ((1, 4), (2, 8))),
        "flags": set_ends((jax.random.randint(seeds[1], (A,), 0, 8) < 7).astype(jnp.int32), jax.random.fold_in(seeds[1], 1), 0, 1),
        "delays": set_ends(jax.random.randint(seeds[2], (A, B), 0, 2 * C), jax.random.fold_in(seeds[2], 1), 0, (2 * C) - 1).astype(jnp.int32),
        "analysis_taps": scatter_about(seeds[3], (TAPS, C), TAPS ** -0.5, 3.0, (), jnp.float32),
        "synthesis_taps": scatter_about(seeds[4], (TAPS, C), TAPS ** -0.5, 3.0, (), jnp.float32),
    }


def forward_table(chan_count):
    indices = jnp.arange(2 * chan_count, dtype=jnp.int32)
    out_chan = indices // 2
    out_part = indices % 2
    in_part = indices // chan_count
    in_sample = indices % chan_count
    wrapped = out_chan[:, None] * in_sample[None, :] % chan_count
    angles = wrapped.astype(jnp.float32) * (2.0 * math.pi / chan_count)
    cosine = jnp.cos(angles)
    sine_part = jnp.sin(angles)
    real_row = jnp.where(in_part[None, :] == 0, cosine, sine_part)
    imag_row = jnp.where(in_part[None, :] == 0, -sine_part, cosine)
    dft_table = jnp.where(out_part[:, None] == 0, real_row, imag_row)
    return (dft_table * (1.0 / math.sqrt(chan_count))).astype(jnp.bfloat16)

def inverse_table(chan_count):
    indices = jnp.arange(2 * chan_count, dtype=jnp.int32)
    out_part = indices // chan_count
    out_sample = indices % chan_count
    in_chan = indices // 2
    in_part = indices % 2
    wrapped = out_sample[:, None] * in_chan[None, :] % chan_count
    angles = wrapped.astype(jnp.float32) * (2.0 * math.pi / chan_count)
    cosine = jnp.cos(angles)
    sine_part = jnp.sin(angles)
    real_row = jnp.where(in_part[None, :] == 0, cosine, -sine_part)
    imag_row = jnp.where(in_part[None, :] == 0, sine_part, cosine)
    dft_table = jnp.where(out_part[:, None] == 0, real_row, imag_row)
    return (dft_table * (1.0 / math.sqrt(chan_count))).astype(jnp.bfloat16)

def steering_weights(delays, channel_list, chan_count):
    odd_steps = 2 * channel_list + 1
    wrapped = odd_steps[:, None, None] * delays[None, :, :] % (2 * chan_count)
    angles = wrapped.astype(jnp.float32) * (math.pi / chan_count)
    cosine = jnp.swapaxes(jnp.cos(angles), 1, 2)
    sine_part = jnp.swapaxes(jnp.sin(angles), 1, 2)
    upper = jnp.concatenate([cosine, sine_part], axis=2)
    lower = jnp.concatenate([-sine_part, cosine], axis=2)
    return jnp.concatenate([upper, lower], axis=1).astype(jnp.bfloat16)

def channelize(block, rim, paired_filter_taps, forward, flag_scale):
    history = paired_filter_taps.shape[0] - 1
    frames = block.shape[1]
    padded = jnp.concatenate([rim.astype(jnp.float32), block.astype(jnp.float32)], axis=1)
    weighted = paired_filter_taps[0] * padded[:, history:history + frames]
    for tap_number in range(1, history + 1):
        weighted = weighted + paired_filter_taps[tap_number] * padded[:, history - tap_number:history - tap_number + frames]
    weighted = weighted.astype(jnp.bfloat16)
    spectra = jnp.einsum('oi,afi->oaf', forward.astype(jnp.float32), weighted.astype(jnp.float32), precision=lax.Precision.HIGHEST)
    spectra = spectra * flag_scale[None, :, None]
    return spectra.astype(jnp.bfloat16).reshape(forward.shape[0] // 2, 2, block.shape[0], frames)

def synthesize_signal(inverse_part, paired_filter_taps):
    history = paired_filter_taps.shape[0] - 1
    frames = inverse_part.shape[1]
    zero_rim = jnp.zeros((inverse_part.shape[0], history, inverse_part.shape[2]), jnp.float32)
    padded = jnp.concatenate([zero_rim, inverse_part.astype(jnp.float32)], axis=1)
    weighted = paired_filter_taps[0] * padded[:, history:history + frames]
    for tap_number in range(1, history + 1):
        weighted = weighted + paired_filter_taps[tap_number] * padded[:, history - tap_number:history - tap_number + frames]
    return weighted.astype(jnp.bfloat16)

def reference(voltages, flags, delays, analysis_taps, synthesis_taps):
    forward = forward_table(C)
    inverse_result = inverse_table(C)
    analysis_both = jnp.concatenate([analysis_taps, analysis_taps], axis=1).astype(jnp.float32)
    synthesis_both = jnp.concatenate([synthesis_taps, synthesis_taps], axis=1).astype(jnp.float32)
    flag_scale = flags.astype(jnp.float32)
    history = TAPS - 1
    zero_rim = jnp.zeros((A, history, 2 * C), jnp.float32)
    spectra = jnp.stack([channelize(voltages[batch_step], zero_rim, analysis_both, forward, flag_scale) for batch_step in range(MB)], axis=1)
    steering_matrix = steering_weights(delays, jnp.arange(C, dtype=jnp.int32), C)

    def per_channel(operands):
        chan_spectra, chan_steer = operands
        blocks = chan_spectra.reshape(MB, 2, A, NBLK, FB).astype(jnp.float32)
        left_part = jnp.concatenate([blocks[:, 0], blocks[:, 1]], axis=-1)
        rotated = jnp.concatenate([blocks[:, 1], -blocks[:, 0]], axis=-1)
        stacked = jnp.concatenate([left_part, rotated], axis=1)
        gram = jnp.einsum('minf,mjnf->nij', stacked, left_part, precision=lax.Precision.HIGHEST)
        gram = (gram * (1.0 / (MB * FB))).reshape(NBLK, 2, A, A)
        flattened_rows = chan_spectra.reshape(MB, 2 * A, NT).astype(jnp.float32)
        formed_beams = jnp.einsum('bi,mif->mbf', chan_steer.astype(jnp.float32), flattened_rows, precision=lax.Precision.HIGHEST)
        formed_beams = (formed_beams * (1.0 / math.sqrt(A))).astype(jnp.bfloat16).reshape(MB, 2, B, NT)
        return (gram, formed_beams)
    vis, formed_all = lax.map(per_channel, (spectra, steering_matrix))
    inverse_wide = inverse_result.astype(jnp.float32)
    beam_list = []
    for batch_step in range(MB):
        beam_spectra = formed_all[:, batch_step].reshape(2 * C, B, NT).astype(jnp.float32)
        inverse_part = jnp.einsum('oi,ibf->bfo', inverse_wide, beam_spectra, precision=lax.Precision.HIGHEST)
        inverse_part = inverse_part.astype(jnp.bfloat16)
        beam_list.append(synthesize_signal(inverse_part, synthesis_both))
    beams = jnp.stack(beam_list, axis=0)
    return (vis, beams)
```

```python
import math

import jax
import jax.numpy as jnp
from jax import lax
from jax.experimental import pallas as pl
from jax.experimental.pallas import tpu as pltpu
from jax.sharding import PartitionSpec as P


A = 512
C = 64
TAPS = 4
FB = 256
MB = 3
RIM = 8


def shifted(value, axis, steps):
    count = lax.axis_size(axis)
    leading, last = (max(0, -steps), min(count, count - steps))
    return lax.ppermute(value, axis, [(source, source + steps) for source in range(leading, last)])


def forward_table(chan_count):
    indices = jnp.arange(2 * chan_count, dtype=jnp.int32)
    out_chan = indices // 2
    out_part = indices % 2
    in_part = indices // chan_count
    in_sample = indices % chan_count
    wrapped = out_chan[:, None] * in_sample[None, :] % chan_count
    angles = wrapped.astype(jnp.float32) * (2.0 * math.pi / chan_count)
    cosine = jnp.cos(angles)
    sine_part = jnp.sin(angles)
    real_row = jnp.where(in_part[None, :] == 0, cosine, sine_part)
    imag_row = jnp.where(in_part[None, :] == 0, -sine_part, cosine)
    dft_table = jnp.where(out_part[:, None] == 0, real_row, imag_row)
    return (dft_table * (1.0 / math.sqrt(chan_count))).astype(jnp.bfloat16)


def inverse_table(chan_count):
    indices = jnp.arange(2 * chan_count, dtype=jnp.int32)
    out_part = indices // chan_count
    out_sample = indices % chan_count
    in_chan = indices // 2
    in_part = indices % 2
    wrapped = out_sample[:, None] * in_chan[None, :] % chan_count
    angles = wrapped.astype(jnp.float32) * (2.0 * math.pi / chan_count)
    cosine = jnp.cos(angles)
    sine_part = jnp.sin(angles)
    real_row = jnp.where(in_part[None, :] == 0, cosine, -sine_part)
    imag_row = jnp.where(in_part[None, :] == 0, sine_part, cosine)
    dft_table = jnp.where(out_part[:, None] == 0, real_row, imag_row)
    return (dft_table * (1.0 / math.sqrt(chan_count))).astype(jnp.bfloat16)


def steering_weights(delays, channel_list, chan_count):
    odd_steps = 2 * channel_list + 1
    wrapped = odd_steps[:, None, None] * delays[None, :, :] % (2 * chan_count)
    angles = wrapped.astype(jnp.float32) * (math.pi / chan_count)
    cosine = jnp.swapaxes(jnp.cos(angles), 1, 2)
    sine_part = jnp.swapaxes(jnp.sin(angles), 1, 2)
    upper = jnp.concatenate([cosine, sine_part], axis=2)
    lower = jnp.concatenate([-sine_part, cosine], axis=2)
    return jnp.concatenate([upper, lower], axis=1).astype(jnp.bfloat16)


def filtered(pad_ref, slot, taps, frames):
    total = taps[0:1] * pad_ref[slot, RIM : RIM + frames]
    for tap_number in range(1, TAPS):
        total = total + taps[tap_number : tap_number + 1] * pad_ref[
            slot, RIM - tap_number : RIM - tap_number + frames
        ]
    return total.astype(jnp.bfloat16)


def channelize_kernel(flags_ref, block_ref, rim_ref, taps_ref, forward_ref, out_ref, pad_ref):
    step = pl.program_id(0)
    groups, tile, rows, frames = out_ref.shape
    taps = taps_ref[...]
    forward = forward_ref[...]
    for slot in range(tile):
        pad_ref[slot, 0:RIM] = rim_ref[slot].astype(jnp.float32)
        pad_ref[slot, RIM : RIM + frames] = block_ref[0, slot].astype(jnp.float32)
        weighted = filtered(pad_ref, slot, taps, frames)
        spectra = lax.dot_general(
            forward, weighted, (((1,), (1,)), ((), ())), preferred_element_type=jnp.float32
        )
        scale = flags_ref[step * tile + slot].astype(jnp.float32)
        spectra = (spectra * scale).astype(jnp.bfloat16)
        out_ref[:, slot] = spectra.reshape(groups, rows, frames)


def channelize(voltages, batch_step, rim, taps, forward, flags, groups):
    antennas, frames, width = voltages.shape[1:]
    rows = width // groups
    tile = 8
    return pl.pallas_call(
        channelize_kernel,
        grid=(antennas // tile,),
        in_specs=[
            pl.BlockSpec(memory_space=pltpu.SMEM),
            pl.BlockSpec((1, tile, frames, width), lambda i: (batch_step, i, 0, 0)),
            pl.BlockSpec((tile, RIM, width), lambda i: (i, 0, 0)),
            pl.BlockSpec((TAPS, width), lambda i: (0, 0)),
            pl.BlockSpec((width, width), lambda i: (0, 0)),
        ],
        out_specs=pl.BlockSpec((groups, tile, rows, frames), lambda i: (0, i, 0, 0)),
        out_shape=jax.ShapeDtypeStruct((groups, antennas, rows, frames), jnp.bfloat16),
        scratch_shapes=[pltpu.VMEM((tile, RIM + frames, width), jnp.float32)],
        cost_estimate=pl.CostEstimate(
            flops=2 * antennas * frames * width * width,
            bytes_accessed=12 * antennas * frames * width,
            transcendentals=0,
        ),
        name="channelize",
    )(flags, voltages, rim, taps, forward)


def synthesize_kernel(*refs):
    piece_ref, tail_ref, taps_ref, inverse_ref = refs[:4]
    out_ref, pad_ref = refs[-2:]
    groups, tile, rows, frames = piece_ref.shape
    taps = taps_ref[...]
    inverse = inverse_ref[...]
    for slot in range(tile):
        block = piece_ref[:, slot].reshape(groups * rows, frames)
        result = lax.dot_general(
            block, inverse, (((0,), (1,)), ((), ())), preferred_element_type=jnp.float32
        )
        pad_ref[slot, 0:RIM] = tail_ref[slot].astype(jnp.float32)
        pad_ref[slot, RIM : RIM + frames] = result.astype(jnp.bfloat16).astype(jnp.float32)
        out_ref[0, slot] = filtered(pad_ref, slot, taps, frames)


def synthesize(piece, tails, taps, inverse_result, batch_step, held):
    groups, beams, rows, frames = piece.shape
    width = groups * rows
    tile = 8
    in_specs = [
        pl.BlockSpec((groups, tile, rows, frames), lambda i: (0, i, 0, 0)),
        pl.BlockSpec((tile, RIM, width), lambda i: (i, 0, 0)),
        pl.BlockSpec((TAPS, width), lambda i: (0, 0)),
        pl.BlockSpec((width, width), lambda i: (0, 0)),
    ]
    operands = [piece, tails, taps, inverse_result]
    aliases = {}
    if held is not None:
        in_specs.append(pl.BlockSpec(memory_space=pl.ANY))
        operands.append(held)
        aliases = {4: 0}
    return pl.pallas_call(
        synthesize_kernel,
        grid=(beams // tile,),
        in_specs=in_specs,
        out_specs=pl.BlockSpec((1, tile, frames, width), lambda i: (batch_step, i, 0, 0)),
        out_shape=jax.ShapeDtypeStruct((MB, beams, frames, width), jnp.bfloat16),
        scratch_shapes=[pltpu.VMEM((tile, RIM + frames, width), jnp.float32)],
        input_output_aliases=aliases,
        cost_estimate=pl.CostEstimate(
            flops=2 * beams * frames * width * width,
            bytes_accessed=12 * beams * frames * width,
            transcendentals=0,
        ),
        name="synthesize",
    )(*operands)


def gram_block(turned):
    left_part = jnp.concatenate([turned[:, 0], turned[:, 1]], axis=-1)
    rotated = jnp.concatenate([turned[:, 1], -turned[:, 0]], axis=-1)
    stacked = jnp.concatenate([left_part, rotated], axis=1)
    return jnp.einsum("cif,cjf->cij", stacked, left_part, preferred_element_type=jnp.float32)


def form_beams(turned, steering_matrix):
    chan_local, parts, antennas, frames = turned.shape
    flattened_rows = turned.reshape(chan_local, parts * antennas, frames)
    formed_beams = jnp.einsum(
        "goq,gqk->gok", steering_matrix, flattened_rows, preferred_element_type=jnp.float32
    )
    formed_beams = (formed_beams * (1.0 / math.sqrt(antennas))).astype(jnp.bfloat16)
    return formed_beams.reshape(chan_local, 2, steering_matrix.shape[1] // 2, frames)


def device_step(voltages, flags, delays, analysis_taps, synthesis_taps):
    groups = lax.axis_size("chan")
    chan_local = C // groups
    beam_local = delays.shape[1] // groups
    frames = voltages.shape[2]
    forward = forward_table(C)
    inverse_result = inverse_table(C)
    analysis_both = jnp.concatenate([analysis_taps, analysis_taps], axis=1)
    synthesis_both = jnp.concatenate([synthesis_taps, synthesis_taps], axis=1)
    channel_list = lax.axis_index("chan") * chan_local + jnp.arange(chan_local, dtype=jnp.int32)
    steering_matrix = steering_weights(delays, channel_list, C)
    spectra_list = []
    for batch_step in range(MB):
        rim = shifted(voltages[batch_step, :, frames - RIM :, :], ("segment", "tm"), 1)
        spectra_list.append(
            channelize(voltages, batch_step, rim, analysis_both, forward, flags, groups)
        )
    gram_total = None
    beams = None
    for batch_step in range(MB):
        arrived = lax.all_to_all(
            spectra_list[batch_step], "chan", split_axis=0, concat_axis=0, tiled=True
        )
        turned = jnp.transpose(
            arrived.reshape(groups, -1, chan_local, 2, frames), (2, 3, 0, 1, 4)
        ).reshape(chan_local, 2, -1, frames)
        gram_piece = gram_block(turned)
        gram_total = gram_piece if batch_step == 0 else gram_total + gram_piece
        formed = form_beams(turned, steering_matrix)
        outgoing = jnp.transpose(
            formed.reshape(chan_local, 2, groups, beam_local, frames), (2, 3, 0, 1, 4)
        ).reshape(groups, beam_local, 2 * chan_local, frames)
        piece = lax.all_to_all(outgoing, "chan", split_axis=0, concat_axis=0, tiled=True)
        last = jnp.einsum(
            "ogr,gbrf->bfo",
            inverse_result.reshape(2 * C, groups, 2 * chan_local),
            piece[:, :, :, frames - RIM :],
            preferred_element_type=jnp.float32,
        ).astype(jnp.bfloat16)
        tails = shifted(last, ("segment", "tm"), 1)
        beams = synthesize(piece, tails, synthesis_both, inverse_result, batch_step, beams)
    vis = (gram_total * (1.0 / (MB * FB))).reshape(chan_local, 1, 2, A, A)
    return (vis, beams)


def solution(mesh):
    placed = (P(None, "chan", ("segment", "tm"), None), P("chan"), P(), P(), P())
    return jax.shard_map(
        device_step,
        mesh=mesh,
        in_specs=placed,
        out_specs=(
            P("chan", ("segment", "tm"), None, None, None),
            P(None, "chan", ("segment", "tm"), None),
        ),
        check_vma=False,
    )
```
